256 devices in a mesh: inline: 16 (over y, z_hi, core), crosslin: 16 (over x, z_lo).
Axes of the slice: x: 4, y: 4, z: 8 (z_hi: 2, z_lo: 4; z = z_hi * 4 + z_lo), core: 2. Of those that a mesh axis runs over, the one named last changes fastest.
Arguments:
- features: bfloat16 [32, 128, 256, 128], P(None, 'inline', 'crosslin'), may hold values from -6 to 6
- first_dilated_weight: bfloat16 [3, 3, 3, 32, 32], replicated, may hold values from -0.3125 to 0.3125
- first_dilated_bias: float32 [32], replicated, may hold values from -3 to 3
- second_dilated_weight: bfloat16 [3, 3, 3, 32, 32], replicated, may hold values from -0.3125 to 0.3125
- second_dilated_bias: float32 [32], replicated, may hold values from -3 to 3
- w_last: bfloat16 [3, 3, 3, 32], replicated, may hold values from -0.4375 to 0.4375
- b_last: float32 [1], replicated, may hold values from -3 to 3
Outputs:
- fault: float32 [128, 256, 128], P('inline', 'crosslin')
The draws below stay inside these ranges and needn't reach their ends.
All inputs are finite; a program needn't handle non-finite values.
Results may differ from the reference program's by a relative error of at most 0.0026.
Values may be sent and summed in bfloat16 or wider, within the bound.
No kernel may reach another device: no remote copies, remote signals or barrier semaphores. Data moves between devices by JAX's collectives and lax.ppermute only.
A program may use at most 64 MiB of HBM per device.

```python
import jax
import jax.numpy as jnp
from jax import lax

C = 32
DILATION_RATE = 8
NX = 128
NY = 256
NZ = 128


def shard_levels(stream_key, dims, split, low, high):
    gain, own = 1.0, jax.random.fold_in(stream_key, 6)
    for position, shards_of in split:
        steps = jnp.exp(jax.random.uniform(jax.random.fold_in(own, position), (shards_of,), jnp.float32, low / len(split), high / len(split)))
        gain = gain * jnp.repeat(steps, dims[position] // shards_of).reshape([-1 if axis == position else 1 for axis in range(len(dims))])
    return gain


def normal_values(own_key, extent, scale, most, cuts=(), dtype=jnp.bfloat16):
    gain = shard_levels(own_key, extent, cuts, -0.22, 0.18) if cuts else 1.0
    entries = jax.random.normal(own_key, extent, jnp.float32) * scale * gain
    return jnp.minimum(jnp.maximum(entries, -most), most).astype(dtype)


def setup_inputs(seed: int = 0) -> dict:
    splits = jax.random.split(jax.random.key(seed), 8)
    return {
        "features": normal_values(splits[0], (C, NX, NY, NZ), 1.0, 6.0, ((1, 16), (2, 16))),
        "first_dilated_weight": normal_values(splits[1], (3, 3, 3, C, C), (27 * C // 2) ** -0.5, 0.3125),
        "first_dilated_bias": normal_values(splits[2], (C,), 0.5, 3.0, (), jnp.float32),
        "second_dilated_weight": normal_values(splits[3], (3, 3, 3, C, C), (27 * C // 2) ** -0.5, 0.3125),
        "second_dilated_bias": normal_values(splits[4], (C,), 0.5, 3.0, (), jnp.float32),
        "w_last": normal_values(splits[5], (3, 3, 3, C), (27 * C // 4) ** -0.5, 0.4375),
        "b_last": normal_values(splits[6], (1,), 1.0, 3.0, (), jnp.float32),
    }


def dilated_result(volume, weight, tap_spacing):
    kernel = jnp.transpose(weight, (3, 4, 0, 1, 2)).astype(jnp.float32)
    result = lax.conv_general_dilated(volume.astype(jnp.float32)[None], kernel, window_strides=(1, 1, 1), padding=[(tap_spacing, tap_spacing)] * 3, rhs_dilation=(tap_spacing, tap_spacing, tap_spacing), dimension_numbers=("NCDHW", "OIDHW", "NCDHW"), precision=lax.Precision.HIGHEST)
    return result[0]


def reference(features, first_dilated_weight, first_dilated_bias, second_dilated_weight, second_dilated_bias, w_last, b_last):
    hidden_first_maps = jax.nn.relu(dilated_result(features, first_dilated_weight, DILATION_RATE) + first_dilated_bias[:, None, None, None]).astype(jnp.bfloat16)
    hidden_second_maps = jax.nn.relu(dilated_result(hidden_first_maps, second_dilated_weight, DILATION_RATE) + second_dilated_bias[:, None, None, None]).astype(jnp.bfloat16)
    logit = dilated_result(hidden_second_maps, w_last[:, :, :, None, :], 1)[0] + b_last[0]
    return jax.nn.sigmoid(logit)
```

```python
import jax
import jax.numpy as jnp
import numpy as np
from jax import lax
from jax.experimental import pallas as pl
from jax.experimental.pallas import tpu as pltpu
from jax.sharding import PartitionSpec as P

S = 8
C = 32
XQ = 16
YQ = 8
Z = 128
HALO = 3
LINE = 4
ROWS = 24
BF = jnp.bfloat16
F32 = jnp.float32


def band_kernel(w1_ref, w2_ref, o1_ref, o2_ref):
    row = lax.broadcasted_iota(jnp.int32, (C, 8 * C), 0)
    lane = lax.broadcasted_iota(jnp.int32, (C, 8 * C), 1)
    repeat = jnp.where(lax.rem(lane, C) == row, 1.0, 0.0).astype(BF)
    block = lane // C
    for w_ref, o_ref in ((w1_ref, o1_ref), (w2_ref, o2_ref)):
        for k in range(9):
            taps = [
                jnp.dot(w_ref[(a * 9 + k) * C : (a * 9 + k + 1) * C, :], repeat, preferred_element_type=F32)
                for a in range(3)
            ]
            for p in range(10):
                value = jnp.zeros((C, 8 * C), F32)
                for a in range(3):
                    if 0 <= p + a - 2 < 8:
                        value = jnp.where(block == p + a - 2, taps[a], value)
                o_ref[p * C : (p + 1) * C, k * 8 * C : (k + 1) * 8 * C] = value.astype(BF)


def z_taps(value):
    lane = lax.broadcasted_iota(jnp.int32, value.shape, 1)
    before = jnp.where(lane < S, 0.0, pltpu.roll(value, S, 1)).astype(BF)
    after = jnp.where(lane >= Z - S, 0.0, pltpu.roll(value, Z - S, 1)).astype(BF)
    return before, value.astype(BF), after


def layers_kernel(
    place_ref, own_ref, low_ref, high_ref, w1_ref, w2_ref, b1_ref, b2_ref, head_ref, out_ref, xs, hs, h2s
):
    block, dx, ext = place_ref[0], place_ref[1], place_ref[2]
    not_first = jnp.where(block > 0, 1.0, 0.0)
    not_last = jnp.where(block < 3, 1.0, 0.0)

    for y in range(-HALO, YQ + HALO):
        for h in range(2):
            part = slice(h * 8, h * 8 + 8)
            if y < 0:
                value = low_ref[y + HALO, part]
            elif y < YQ:
                value = own_ref[y // 2, part, y % 2]
            else:
                value = high_ref[y - YQ, part]
            for dz, v in enumerate(z_taps(value.reshape(8 * C, Z).astype(F32))):
                if y <= 4:
                    xs[h, y + 3, dz, :, 0:Z] = v
                if y >= 3:
                    xs[h, y - 3, dz, :, Z : 2 * Z] = v

    def layer(source, t, w_ref, b_ref):
        first = jnp.dot(
            w_ref[C : 10 * C, :], source[0, pl.ds(t, 3)].reshape(9 * 8 * C, 2 * Z), preferred_element_type=F32
        )
        second = jnp.dot(
            w_ref[0 : 9 * C, :], source[1, pl.ds(t, 3)].reshape(9 * 8 * C, 2 * Z), preferred_element_type=F32
        )
        total = jnp.concatenate(
            [first[: 7 * C], first[7 * C :] + second[: 2 * C], second[2 * C :]], axis=0
        )
        return jnp.maximum(total + b_ref[...], 0.0)

    @pl.loop(0, 6)
    def _(t):
        value = layer(xs, t, w1_ref, b1_ref)
        left = value[:, :Z] * jnp.where(t < 2, not_first, 1.0)
        right = value[:, Z:] * jnp.where(t > 3, not_last, 1.0)
        for h in range(2):
            part = slice(h * 8 * C, (h + 1) * 8 * C)
            lefts, rights = z_taps(left[part]), z_taps(right[part])
            for dz in range(3):
                hs[h, t, dz, :, 0:Z] = lefts[dz]
                hs[h, t + 1, dz, :, Z : 2 * Z] = rights[dz]

            @pl.when(t == 5)
            def _():
                for dz in range(3):
                    hs[h, 0, dz, :, Z : 2 * Z] = lefts[dz]

            @pl.when(t == 0)
            def _():
                for dz in range(3):
                    hs[h, 6, dz, :, 0:Z] = rights[dz]

    h2s[0] = jnp.zeros((YQ + 2, C, Z), BF)
    h2s[XQ + 1] = jnp.zeros((YQ + 2, C, Z), BF)

    @pl.loop(0, 5)
    def _(t):
        value = layer(hs, t, w2_ref, b2_ref)
        left = value[:, :Z] * jnp.where(t < 1, not_first, 1.0)
        right = value[:, Z:] * jnp.where(t > 3, not_last, 1.0)
        h2s[1 : XQ + 1, t] = left.astype(BF).reshape(XQ, C, Z)
        h2s[1 : XQ + 1, t + 5] = right.astype(BF).reshape(XQ, C, Z)

    lane = lax.broadcasted_iota(jnp.int32, (ROWS, Z), 1)
    for l in range(0, LINE, 2):

        @pl.loop(0, XQ // 2)
        def _(pair):
            halves = ([], [])
            for sub in range(2):
                x = pair * 2 + sub + 1
                columns = []
                for k in (l, l + 1):
                    y = 2 * k + 1
                    columns.append(
                        jnp.concatenate(
                            [h2s[x + dx * e, at] for e in range(2) for at in (y, y + 1, y + ext)], axis=0
                        )
                    )
                sums = jnp.dot(
                    head_ref[...], jnp.concatenate(columns, axis=1), preferred_element_type=F32
                )
                for k in range(2):
                    part = sums[:, k * Z : (k + 1) * Z]
                    before = jnp.where(lane < 1, 0.0, pltpu.roll(part[:ROWS], 1, 1))
                    after = jnp.where(lane >= Z - 1, 0.0, pltpu.roll(part[2 * ROWS :], Z - 1, 1))
                    halves[k].append(part[ROWS : 2 * ROWS] + before + after)
            for k in range(2):
                at = pl.multiple_of(((l + k) * XQ + pair * 2) * ROWS, 16)
                out_ref[pl.ds(at, 2 * ROWS), :] = jnp.concatenate(halves[k], axis=0).astype(BF)


def finish_kernel(back_ref, pick_ref, b_ref, out_ref):
    totals = [None] * S
    for r in range(S):
        sums = jnp.dot(
            pick_ref[...], back_ref[r * S * ROWS : (r + 1) * S * ROWS, :], preferred_element_type=F32
        )
        for a in range(3):
            to = (r - (a - 1)) % S
            part = sums[a * 16 : (a + 1) * 16]
            totals[to] = part if totals[to] is None else totals[to] + part
    for x in range(S):
        out_ref[x] = 1.0 / (1.0 + jnp.exp(-(totals[x] + b_ref[0])))


def pick_matrix():
    pick = np.zeros((3, 2, S, S, ROWS), np.float32)
    for a in range(3):
        for e in range(2):
            for y in range(S):
                for b in range(3):
                    pick[a, e, y, (y + b - 1) % S, e * 9 + a * 3 + b] = 1.0
    return pick.reshape(3 * 2 * S, S * ROWS).astype(jnp.bfloat16)


def head_matrix(w_last, r, s):
    a = jnp.arange(3)[None, :, None]
    b = jnp.arange(3)[None, None, :]
    e = jnp.arange(2)[:, None, None]
    x_from = jnp.where(((a == 2) & (r == 0)) | ((a == 0) & (r == S - 1)), 1, 0)
    up = (b == 2) & (s == 0)
    down = (b == 0) & (s == S - 1)
    y_from = jnp.where(up, e + 1, jnp.where(down, jnp.where(e == 0, 2, 0), e))
    source = x_from * 3 + y_from
    mask = (source[..., None] == jnp.arange(6)).astype(BF)
    weight = jnp.transpose(w_last, (2, 0, 1, 3))
    full = mask[None, :, :, :, :, None] * weight[:, None, :, :, None, :]
    full = full.reshape(3, 18, 6 * C)
    return jnp.pad(full, ((0, 0), (0, ROWS - 18), (0, 0))).reshape(3 * ROWS, 6 * C)


VMEM = pl.BlockSpec(memory_space=pltpu.VMEM)
SMEM = pl.BlockSpec(memory_space=pltpu.SMEM)


def make_body(groups, steps):
    axes = ("inline", "crosslin")

    def swap(value):
        return lax.all_to_all(value, axes, 0, 0, tiled=True, axis_index_groups=groups)

    def body(features, w1, b1, w2, b2, w_last, b_last):
        j = lax.axis_index("crosslin")
        block = j // LINE
        k = lax.rem(j, LINE) * XQ + lax.axis_index("inline")
        r, s = k // S, lax.rem(k, S)

        send = features.reshape(C, S, 2, S, Z).transpose(1, 3, 2, 0, 4).reshape(S * S, 2 * C, Z)
        own = swap(send).reshape(LINE, XQ, 2, C, Z)
        first = jnp.stack([own[0, :, 0], own[0, :, 1], own[1, :, 0]])
        last = jnp.stack([own[2, :, 1], own[3, :, 0], own[3, :, 1]])
        ends = steps - LINE
        high = lax.ppermute(first, "crosslin", [(i + LINE, i) for i in range(ends)])
        low = lax.ppermute(last, "crosslin", [(i, i + LINE) for i in range(ends)])

        band1, band2 = pl.pallas_call(
            band_kernel,
            out_shape=[jax.ShapeDtypeStruct((10 * C, 9 * 8 * C), BF)] * 2,
            in_specs=[VMEM] * 2,
            out_specs=[VMEM] * 2,
            cost_estimate=pl.CostEstimate(flops=60000000, bytes_accessed=3200000, transcendentals=0),
        )(w1.reshape(27 * C, C), w2.reshape(27 * C, C))

        dx = jnp.where(r == 0, 1, jnp.where(r == S - 1, -1, 0))
        ext = jnp.where(s == S - 1, -1, 2)
        place = jnp.stack([block, dx, ext, 0]).astype(jnp.int32)
        bias1 = jnp.tile(b1, XQ)[:, None]
        bias2 = jnp.tile(b2, XQ)[:, None]
        parts = pl.pallas_call(
            layers_kernel,
            out_shape=jax.ShapeDtypeStruct((S * S * ROWS, Z), BF),
            in_specs=[SMEM] + [VMEM] * 8,
            out_specs=VMEM,
            scratch_shapes=[
                pltpu.VMEM((2, 8, 3, 8 * C, 2 * Z), BF),
                pltpu.VMEM((2, 7, 3, 8 * C, 2 * Z), BF),
                pltpu.VMEM((XQ + 2, YQ + 2, C, Z), BF),
            ],
            compiler_params=pltpu.CompilerParams(vmem_limit_bytes=48 << 20),
            cost_estimate=pl.CostEstimate(flops=8000000000, bytes_accessed=6000000, transcendentals=0),
        )(place, own, low, high, band1, band2, bias1, bias2, head_matrix(w_last, r, s))

        back = swap(parts.reshape(S * S, ROWS, Z)).reshape(S * S * ROWS, Z)
        return pl.pallas_call(
            finish_kernel,
            out_shape=jax.ShapeDtypeStruct((S, 2 * S, Z), F32),
            in_specs=[VMEM, VMEM, SMEM],
            out_specs=VMEM,
        )(back, jnp.asarray(pick_matrix()), b_last)

    return body


def solution(mesh):
    rows, steps = mesh.shape["inline"], mesh.shape["crosslin"]
    groups = [
        [i * steps + x * LINE + l for l in range(LINE) for i in range(rows)] for x in range(steps // LINE)
    ]
    return jax.shard_map(
        make_body(groups, steps),
        mesh=mesh,
        in_specs=(P(None, "inline", "crosslin", None), P(), P(), P(), P(), P(), P()),
        out_specs=P("inline", "crosslin", None),
        check_vma=False,
    )
```

```python
import jax
import jax.numpy as jnp
import numpy as np
from jax import lax
from jax.experimental import pallas as pl
from jax.experimental.pallas import tpu as pltpu
from jax.sharding import PartitionSpec as P

S = 8
C = 32
XQ = 16
YQ = 8
Z = 128
HALO = 3
LINE = 4
HALF = 8 * C
ROWS = 24
BF = jnp.bfloat16
F32 = jnp.float32


def band_kernel(w1_ref, w2_ref, o1_ref, o2_ref):
    row = lax.broadcasted_iota(jnp.int32, (C, HALF), 0)
    lane = lax.broadcasted_iota(jnp.int32, (C, HALF), 1)
    repeat = jnp.where(lax.rem(lane, C) == row, 1.0, 0.0).astype(BF)
    block = lane // C
    for w_ref, o_ref in ((w1_ref, o1_ref), (w2_ref, o2_ref)):
        for dy in range(3):
            for dz in range(3):
                taps = [
                    jnp.dot(
                        w_ref[((a * 3 + dy) * 3 + dz) * C : ((a * 3 + dy) * 3 + dz + 1) * C, :],
                        repeat,
                        preferred_element_type=F32,
                    )
                    for a in range(3)
                ]
                for p in range(10):
                    value = jnp.zeros((C, HALF), F32)
                    for a in range(3):
                        if 0 <= p + a - 2 < 8:
                            value = jnp.where(block == p + a - 2, taps[a], value)
                    at = (dz * 10 + p) * C
                    o_ref[at : at + C, dy * HALF : (dy + 1) * HALF] = value.astype(BF)


def layer_pair(fetch, first, second, w_ref, b_ref, sums, keep):
    for h in range(2):
        taps = jnp.concatenate(
            [w_ref[(dz * 10 + 1 - h) * C : (dz * 10 + 10 - h) * C, :] for dz in range(3)], axis=0
        )
        window = jnp.concatenate(
            [
                jnp.concatenate([fetch(first + dy, h), fetch(second + dy, h)], axis=1)
                for dy in (-1, 0, 1)
            ],
            axis=0,
        )
        sums[h] = jnp.dot(taps, window, preferred_element_type=F32)
    lane = lax.broadcasted_iota(jnp.int32, (C, Z), 1)
    bias = b_ref[...]
    for x in range(XQ):
        for side, y in enumerate((first, second)):
            lanes = slice(side * Z, (side + 1) * Z)
            parts = []
            for dz in range(3):
                part = None
                if x <= 8:
                    part = sums[0, (dz * 9 + x) * C : (dz * 9 + x + 1) * C, lanes]
                if x >= 7:
                    other = sums[1, (dz * 9 + x - 7) * C : (dz * 9 + x - 6) * C, lanes]
                    part = other if part is None else part + other
                parts.append(part)
            total = parts[1] + jnp.where(lane < S, 0.0, pltpu.roll(parts[0], S, 1))
            total = total + jnp.where(lane >= Z - S, 0.0, pltpu.roll(parts[2], Z - S, 1))
            keep(x, y, jnp.maximum(total + bias, 0.0))


def inner_kernel(own_ref, w1_ref, w2_ref, b1_ref, b2_ref, one_ref, two_ref, sums):
    def features(y, h):
        return own_ref[y // 2, h * 8 : h * 8 + 8, y % 2].reshape(HALF, Z)

    def hidden(y, h):
        return one_ref[y - 1, h * HALF : (h + 1) * HALF, :]

    def keep_one(x, y, value):
        one_ref[y - 1, x * C : (x + 1) * C, :] = value.astype(BF)

    def keep_two(x, y, value):
        two_ref[x, y - 2] = value.astype(BF)

    for y in range(1, 4):
        layer_pair(features, y, y + 3, w1_ref, b1_ref, sums, keep_one)
    for y in range(2, 4):
        layer_pair(hidden, y, y + 2, w2_ref, b2_ref, sums, keep_two)


def outer_kernel(
    place_ref, own_ref, low_ref, high_ref, one_ref, two_ref, w1_ref, w2_ref, b1_ref, b2_ref, head_ref, out_ref,
    edge, h2s, sums,
):
    block, dx, ext = place_ref[0], place_ref[1], place_ref[2]
    not_first = jnp.where(block > 0, 1.0, 0.0)
    not_last = jnp.where(block < 3, 1.0, 0.0)

    def inside(y, value):
        return value * not_first if y < 0 else value * not_last if y >= YQ else value

    def features(y, h):
        part = slice(h * 8, h * 8 + 8)
        if y < 0:
            value = low_ref[y + HALO, part]
        elif y < YQ:
            value = own_ref[y // 2, part, y % 2]
        else:
            value = high_ref[y - YQ, part]
        return value.reshape(HALF, Z)

    def hidden(y, h):
        part = slice(h * HALF, (h + 1) * HALF)
        if 1 <= y <= 6:
            return one_ref[y - 1, part, :]
        return edge[y + 2 if y < 1 else y - 4, part, :]

    def keep_one(x, y, value):
        edge[y + 2 if y < 1 else y - 4, x * C : (x + 1) * C, :] = inside(y, value).astype(BF)

    def keep_two(x, y, value):
        h2s[x + 1, y + 1] = inside(y, value).astype(BF)

    for y in range(-2, 1):
        layer_pair(features, y, y + 9, w1_ref, b1_ref, sums, keep_one)
    h2s[0] = jnp.zeros((YQ + 2, C, Z), BF)
    h2s[XQ + 1] = jnp.zeros((YQ + 2, C, Z), BF)
    for x in range(XQ):
        h2s[x + 1, 3:7] = two_ref[x]
    for y in range(-1, 2):
        layer_pair(hidden, y, y + 7, w2_ref, b2_ref, sums, keep_two)

    lane = lax.broadcasted_iota(jnp.int32, (ROWS, Z), 1)
    for l in range(0, LINE, 2):
        for pair in range(0, XQ, 2):
            halves = ([], [])
            for x in (pair + 1, pair + 2):
                columns = []
                for k in (l, l + 1):
                    y = 2 * k + 1
                    columns.append(
                        jnp.concatenate(
                            [h2s[at_x, at] for at_x in (x, x + dx) for at in (y, y + 1, y + ext)], axis=0
                        )
                    )
                both = jnp.dot(head_ref[...], jnp.concatenate(columns, axis=1), preferred_element_type=F32)
                for k in range(2):
                    part = both[:, k * Z : (k + 1) * Z]
                    before = jnp.where(lane < 1, 0.0, pltpu.roll(part[:ROWS], 1, 1))
                    after = jnp.where(lane >= Z - 1, 0.0, pltpu.roll(part[2 * ROWS :], Z - 1, 1))
                    halves[k].append(part[ROWS : 2 * ROWS] + before + after)
            for k in range(2):
                at = ((l + k) * XQ + pair) * ROWS
                out_ref[at : at + 2 * ROWS, :] = jnp.concatenate(halves[k], axis=0).astype(BF)


def finish_kernel(back_ref, pick_ref, b_ref, out_ref):
    totals = [None] * S
    for r in range(S):
        sums = jnp.dot(
            pick_ref[...], back_ref[r * S * ROWS : (r + 1) * S * ROWS, :], preferred_element_type=F32
        )
        for a in range(3):
            to = (r - (a - 1)) % S
            part = sums[a * 16 : (a + 1) * 16]
            totals[to] = part if totals[to] is None else totals[to] + part
    for x in range(S):
        out_ref[x] = 1.0 / (1.0 + jnp.exp(-(totals[x] + b_ref[0])))


def pick_matrix():
    pick = np.zeros((3, 2, S, S, ROWS), np.float32)
    for a in range(3):
        for e in range(2):
            for y in range(S):
                for b in range(3):
                    pick[a, e, y, (y + b - 1) % S, e * 9 + a * 3 + b] = 1.0
    return pick.reshape(3 * 2 * S, S * ROWS).astype(jnp.bfloat16)


def head_matrix(w_last, r, s):
    a = jnp.arange(3)[None, :, None]
    b = jnp.arange(3)[None, None, :]
    e = jnp.arange(2)[:, None, None]
    x_from = jnp.where(((a == 2) & (r == 0)) | ((a == 0) & (r == S - 1)), 1, 0)
    up = (b == 2) & (s == 0)
    down = (b == 0) & (s == S - 1)
    y_from = jnp.where(up, e + 1, jnp.where(down, jnp.where(e == 0, 2, 0), e))
    source = x_from * 3 + y_from
    mask = (source[..., None] == jnp.arange(6)).astype(BF)
    weight = jnp.transpose(w_last, (2, 0, 1, 3))
    full = mask[None, :, :, :, :, None] * weight[:, None, :, :, None, :]
    full = full.reshape(3, 18, 6 * C)
    return jnp.pad(full, ((0, 0), (0, ROWS - 18), (0, 0))).reshape(3 * ROWS, 6 * C)


VMEM = pl.BlockSpec(memory_space=pltpu.VMEM)
SMEM = pl.BlockSpec(memory_space=pltpu.SMEM)


def make_body(groups, steps):
    axes = ("inline", "crosslin")

    def swap(value):
        return lax.all_to_all(value, axes, 0, 0, tiled=True, axis_index_groups=groups)

    def body(features, w1, b1, w2, b2, w_last, b_last):
        j = lax.axis_index("crosslin")
        block = j // LINE
        k = lax.rem(j, LINE) * XQ + lax.axis_index("inline")
        r, s = k // S, lax.rem(k, S)

        send = features.reshape(C, S, 2, S, Z).transpose(1, 3, 2, 0, 4).reshape(S * S, 2 * C, Z)
        own = swap(send)
        band1, band2 = pl.pallas_call(
            band_kernel,
            out_shape=[jax.ShapeDtypeStruct((30 * C, 3 * HALF), BF)] * 2,
            in_specs=[VMEM] * 2,
            out_specs=[VMEM] * 2,
            compiler_params=pltpu.CompilerParams(vmem_limit_bytes=16 << 20),
            cost_estimate=pl.CostEstimate(flops=60000000, bytes_accessed=3200000, transcendentals=0),
        )(w1.reshape(27 * C, C), w2.reshape(27 * C, C))
        dx = jnp.where(r == 0, 1, jnp.where(r == S - 1, -1, 0))
        ext = jnp.where(s == S - 1, -1, 2)
        place = jnp.stack([block, dx, ext, 0]).astype(jnp.int32)
        head = head_matrix(w_last, r, s)
        bias1, bias2 = (jnp.broadcast_to(b[:, None], (C, Z)) for b in (b1, b2))
        own, band1, band2, place, head, bias1, bias2 = lax.optimization_barrier(
            (own, band1, band2, place, head, bias1, bias2)
        )

        own = own.reshape(LINE, XQ, 2, C, Z)
        first = jnp.stack([own[0, :, 0], own[0, :, 1], own[1, :, 0]])
        last = jnp.stack([own[2, :, 1], own[3, :, 0], own[3, :, 1]])
        ends = steps - LINE
        high = lax.ppermute(first, "crosslin", [(i + LINE, i) for i in range(ends)])
        low = lax.ppermute(last, "crosslin", [(i, i + LINE) for i in range(ends)])

        one, two = pl.pallas_call(
            inner_kernel,
            out_shape=[jax.ShapeDtypeStruct((6, XQ * C, Z), BF), jax.ShapeDtypeStruct((XQ, 4, C, Z), BF)],
            in_specs=[VMEM] * 5,
            out_specs=[VMEM] * 2,
            scratch_shapes=[pltpu.VMEM((2, 27 * C, 2 * Z), F32)],
            compiler_params=pltpu.CompilerParams(vmem_limit_bytes=32 << 20),
            cost_estimate=pl.CostEstimate(flops=4000000000, bytes_accessed=6000000, transcendentals=0),
        )(own, band1, band2, bias1, bias2)
        parts = pl.pallas_call(
            outer_kernel,
            out_shape=jax.ShapeDtypeStruct((S * S * ROWS, Z), BF),
            in_specs=[SMEM] + [VMEM] * 10,
            out_specs=VMEM,
            scratch_shapes=[
                pltpu.VMEM((6, XQ * C, Z), BF),
                pltpu.VMEM((XQ + 2, YQ + 2, C, Z), BF),
                pltpu.VMEM((2, 27 * C, 2 * Z), F32),
            ],
            compiler_params=pltpu.CompilerParams(vmem_limit_bytes=32 << 20),
            cost_estimate=pl.CostEstimate(flops=5000000000, bytes_accessed=7000000, transcendentals=0),
        )(place, own, low, high, one, two, band1, band2, bias1, bias2, head)

        back = swap(parts.reshape(S * S, ROWS, Z)).reshape(S * S * ROWS, Z)
        return pl.pallas_call(
            finish_kernel,
            out_shape=jax.ShapeDtypeStruct((S, 2 * S, Z), F32),
            in_specs=[VMEM, VMEM, SMEM],
            out_specs=VMEM,
            compiler_params=pltpu.CompilerParams(vmem_limit_bytes=16 << 20),
        )(back, jnp.asarray(pick_matrix()), b_last)

    return body


def solution(mesh):
    rows, steps = mesh.shape["inline"], mesh.shape["crosslin"]
    groups = [
        [i * steps + x * LINE + l for l in range(LINE) for i in range(rows)] for x in range(steps // LINE)
    ]
    return jax.shard_map(
        make_body(groups, steps),
        mesh=mesh,
        in_specs=(P(None, "inline", "crosslin", None), P(), P(), P(), P(), P(), P()),
        out_specs=P("inline", "crosslin", None),
        check_vma=False,
    )
```

```python
import jax
import jax.numpy as jnp
import numpy as np
from jax import lax
from jax.experimental import pallas as pl
from jax.experimental.pallas import tpu as pltpu
from jax.sharding import PartitionSpec as P

S = 8
C = 32
XQ = 16
YQ = 8
Z = 128
LINE = 4
HALF = 8 * C
ROWS = 24
BF = jnp.bfloat16
F32 = jnp.float32


def band_kernel(w1_ref, w2_ref, o1_ref, o2_ref):
    row = lax.broadcasted_iota(jnp.int32, (C, HALF), 0)
    lane = lax.broadcasted_iota(jnp.int32, (C, HALF), 1)
    repeat = jnp.where(lax.rem(lane, C) == row, 1.0, 0.0).astype(BF)
    block = lane // C
    for w_ref, o_ref in ((w1_ref, o1_ref), (w2_ref, o2_ref)):
        for dy in range(3):
            for dz in range(3):
                taps = [
                    jnp.dot(
                        w_ref[((a * 3 + dy) * 3 + dz) * C : ((a * 3 + dy) * 3 + dz + 1) * C, :],
                        repeat,
                        preferred_element_type=F32,
                    )
                    for a in range(3)
                ]
                for p in range(10):
                    value = jnp.zeros((C, HALF), F32)
                    for a in range(3):
                        if 0 <= p + a - 2 < 8:
                            value = jnp.where(block == p + a - 2, taps[a], value)
                    at = (dz * 10 + p) * C
                    o_ref[at : at + C, dy * HALF : (dy + 1) * HALF] = value.astype(BF)


def layer_at(windows, w_ref, b_ref, sums, keep):
    wide = len(windows) * Z
    for h in range(2):
        taps = jnp.concatenate(
            [w_ref[(dz * 10 + 1 - h) * C : (dz * 10 + 10 - h) * C, :] for dz in range(3)], axis=0
        )
        window = jnp.concatenate(
            [jnp.concatenate([at(dy, h) for at in windows], axis=1) for dy in (-1, 0, 1)], axis=0
        )
        sums[h, :, 0:wide] = jnp.dot(taps, window, preferred_element_type=F32)
    lane = lax.broadcasted_iota(jnp.int32, (C, Z), 1)
    bias = b_ref[...]
    for x in range(XQ):
        for side in range(len(windows)):
            lanes = slice(side * Z, (side + 1) * Z)
            parts = []
            for dz in range(3):
                part = None
                if x <= 8:
                    part = sums[0, (dz * 9 + x) * C : (dz * 9 + x + 1) * C, lanes]
                if x >= 7:
                    other = sums[1, (dz * 9 + x - 7) * C : (dz * 9 + x - 6) * C, lanes]
                    part = other if part is None else part + other
                parts.append(part)
            total = parts[1] + jnp.where(lane < S, 0.0, pltpu.roll(parts[0], S, 1))
            total = total + jnp.where(lane >= Z - S, 0.0, pltpu.roll(parts[2], Z - S, 1))
            keep(x, side, jnp.maximum(total + bias, 0.0))


def layer_pair(fetch, first, second, w_ref, b_ref, sums, keep):
    pair = (first, second)
    layer_at(
        [lambda dy, h, y=y: fetch(y + dy, h) for y in pair],
        w_ref, b_ref, sums, lambda x, side, value: keep(x, pair[side], value),
    )


def inner_kernel(own_ref, w1_ref, w2_ref, b1_ref, b2_ref, one_ref, two_ref, sums):
    def features(y, h):
        return own_ref[y // 2, h * 8 : h * 8 + 8, y % 2].reshape(HALF, Z)

    def hidden(y, h):
        return one_ref[y - 1, h * HALF : (h + 1) * HALF, :]

    def keep_one(x, y, value):
        one_ref[y - 1, x * C : (x + 1) * C, :] = value.astype(BF)

    def keep_two(x, y, value):
        two_ref[x, y - 2] = value.astype(BF)

    for y in range(1, 4):
        layer_pair(features, y, y + 3, w1_ref, b1_ref, sums, keep_one)
    for y in range(2, 4):
        layer_pair(hidden, y, y + 2, w2_ref, b2_ref, sums, keep_two)


def outer_kernel(
    place_ref, own_ref, low_ref, high_ref, far_ref, one_ref, two_ref, w1_ref, w2_ref, b1_ref, b2_ref, head_ref,
    out_ref, ends, edge, h2s, sums,
):
    block, dx, ext, start = place_ref[0], place_ref[1], place_ref[2], place_ref[3]
    not_first = jnp.where(block > 0, 1.0, 0.0)
    not_last = jnp.where(block < 3, 1.0, 0.0)
    ninth = jnp.where(start == 0, not_first, not_last)

    def inside(y, value):
        return value * not_first if y < 0 else value * not_last if y >= YQ else value

    def slot(y):
        return y + 3 if y < 0 else y - 5

    for x in range(XQ):
        ends[0, x] = far_ref[x]
        ends[5, x] = far_ref[x]
        for y in range(2):
            ends[1 + y, x] = low_ref[x, y]
            ends[3 + y, x] = high_ref[x, y]

    def features(y, h):
        part = slice(h * 8, h * 8 + 8)
        value = own_ref[y // 2, part, y % 2] if 0 <= y < YQ else ends[slot(y), part]
        return value.reshape(HALF, Z)

    def hidden(y, h):
        part = slice(h * HALF, (h + 1) * HALF)
        if 1 <= y <= 6:
            return one_ref[y - 1, part, :]
        return edge[y + 2 if y < 1 else y - 4, part, :]

    def keep_one(x, y, value):
        edge[y + 2 if y < 1 else y - 4, x * C : (x + 1) * C, :] = inside(y, value).astype(BF)

    def keep_two(x, y, value):
        h2s[x + 1, y + 1] = value.astype(BF)

    def keep_one_ninth(x, side, value):
        edge[jnp.where(start == 0, 0, 5), x * C : (x + 1) * C, :] = (value * ninth).astype(BF)

    def keep_two_ninth(x, side, value):
        h2s[x + 1, jnp.where(start == 0, 0, 9)] = (value * ninth).astype(BF)

    for y in (-1, 0):
        layer_pair(features, y, y + 8, w1_ref, b1_ref, sums, keep_one)
    layer_at(
        [lambda dy, h: ends[start + 1 + dy, h * 8 : h * 8 + 8].reshape(HALF, Z)],
        w1_ref, b1_ref, sums, keep_one_ninth,
    )
    h2s[0] = jnp.zeros((YQ + 2, C, Z), BF)
    h2s[XQ + 1] = jnp.zeros((YQ + 2, C, Z), BF)
    for x in range(XQ):
        h2s[x + 1, 3:7] = two_ref[x]
    for y in (0, 1):
        layer_pair(hidden, y, y + 6, w2_ref, b2_ref, sums, keep_two)
    layer_at(
        [lambda dy, h: edge[start + 1 + dy, h * HALF : (h + 1) * HALF, :]],
        w2_ref, b2_ref, sums, keep_two_ninth,
    )

    lane = lax.broadcasted_iota(jnp.int32, (ROWS, Z), 1)
    for l in range(0, LINE, 2):
        for pair in range(0, XQ, 2):
            halves = ([], [])
            for x in (pair + 1, pair + 2):
                columns = []
                for k in (l, l + 1):
                    y = 2 * k + 1
                    columns.append(
                        jnp.concatenate(
                            [h2s[at_x, at] for at_x in (x, x + dx) for at in (y, y + 1, y + ext)], axis=0
                        )
                    )
                both = jnp.dot(head_ref[...], jnp.concatenate(columns, axis=1), preferred_element_type=F32)
                for k in range(2):
                    part = both[:, k * Z : (k + 1) * Z]
                    before = jnp.where(lane < 1, 0.0, pltpu.roll(part[:ROWS], 1, 1))
                    after = jnp.where(lane >= Z - 1, 0.0, pltpu.roll(part[2 * ROWS :], Z - 1, 1))
                    halves[k].append(part[ROWS : 2 * ROWS] + before + after)
            for k in range(2):
                at = ((l + k) * XQ + pair) * ROWS
                out_ref[at : at + 2 * ROWS, :] = jnp.concatenate(halves[k], axis=0).astype(BF)


def finish_kernel(back_ref, pick_ref, b_ref, out_ref):
    totals = [None] * S
    for r in range(S):
        sums = jnp.dot(
            pick_ref[...], back_ref[r * S * ROWS : (r + 1) * S * ROWS, :], preferred_element_type=F32
        )
        for a in range(3):
            to = (r - (a - 1)) % S
            part = sums[a * 16 : (a + 1) * 16]
            totals[to] = part if totals[to] is None else totals[to] + part
    for x in range(S):
        out_ref[x] = 1.0 / (1.0 + jnp.exp(-(totals[x] + b_ref[0])))


def pick_matrix():
    pick = np.zeros((3, 2, S, S, ROWS), np.float32)
    for a in range(3):
        for e in range(2):
            for y in range(S):
                for b in range(3):
                    pick[a, e, y, (y + b - 1) % S, e * 9 + a * 3 + b] = 1.0
    return pick.reshape(3 * 2 * S, S * ROWS).astype(jnp.bfloat16)


def head_matrix(w_last, r, s):
    a = jnp.arange(3)[None, :, None]
    b = jnp.arange(3)[None, None, :]
    e = jnp.arange(2)[:, None, None]
    x_from = jnp.where(((a == 2) & (r == 0)) | ((a == 0) & (r == S - 1)), 1, 0)
    up = (b == 2) & (s == 0)
    down = (b == 0) & (s == S - 1)
    y_from = jnp.where(up, e + 1, jnp.where(down, jnp.where(e == 0, 2, 0), e))
    source = x_from * 3 + y_from
    mask = (source[..., None] == jnp.arange(6)).astype(BF)
    weight = jnp.transpose(w_last, (2, 0, 1, 3))
    full = mask[None, :, :, :, :, None] * weight[:, None, :, :, None, :]
    full = full.reshape(3, 18, 6 * C)
    return jnp.pad(full, ((0, 0), (0, ROWS - 18), (0, 0))).reshape(3 * ROWS, 6 * C)


VMEM = pl.BlockSpec(memory_space=pltpu.VMEM)
SMEM = pl.BlockSpec(memory_space=pltpu.SMEM)


def make_body(groups, far_pairs, steps):
    axes = ("inline", "crosslin")

    def swap(value):
        return lax.all_to_all(value, axes, 0, 0, tiled=True, axis_index_groups=groups)

    def body(features, w1, b1, w2, b2, w_last, b_last):
        j = lax.axis_index("crosslin")
        block = j // LINE
        k = lax.rem(j, LINE) * XQ + lax.axis_index("inline")
        r, s = k // S, lax.rem(k, S)

        send = features.reshape(C, S, 2, S, Z).transpose(1, 3, 2, 0, 4).reshape(S * S, 2 * C, Z)
        own = swap(send)
        band1, band2 = pl.pallas_call(
            band_kernel,
            out_shape=[jax.ShapeDtypeStruct((30 * C, 3 * HALF), BF)] * 2,
            in_specs=[VMEM] * 2,
            out_specs=[VMEM] * 2,
            compiler_params=pltpu.CompilerParams(vmem_limit_bytes=16 << 20),
            cost_estimate=pl.CostEstimate(flops=60000000, bytes_accessed=3200000, transcendentals=0),
        )(w1.reshape(27 * C, C), w2.reshape(27 * C, C))
        dx = jnp.where(r == 0, 1, jnp.where(r == S - 1, -1, 0))
        ext = jnp.where(s == S - 1, -1, 2)
        place = jnp.stack([block, dx, ext, jnp.where(s == S - 1, 0, 3)]).astype(jnp.int32)
        head = head_matrix(w_last, r, s)
        bias1, bias2 = (jnp.broadcast_to(b[:, None], (C, Z)) for b in (b1, b2))
        own, band1, band2, place, head, bias1, bias2 = lax.optimization_barrier(
            (own, band1, band2, place, head, bias1, bias2)
        )

        own = own.reshape(LINE, XQ, 2, C, Z)
        far = jnp.where(s == S - 1, own[2, :, 1], own[1, :, 0])
        high = lax.ppermute(own[0], "crosslin", [(i + LINE, i) for i in range(steps - LINE)])
        low = lax.ppermute(own[3], "crosslin", [(i, i + LINE) for i in range(steps - LINE)])
        far = lax.ppermute(far, axes, far_pairs)

        one, two = pl.pallas_call(
            inner_kernel,
            out_shape=[jax.ShapeDtypeStruct((6, XQ * C, Z), BF), jax.ShapeDtypeStruct((XQ, 4, C, Z), BF)],
            in_specs=[VMEM] * 5,
            out_specs=[VMEM] * 2,
            scratch_shapes=[pltpu.VMEM((2, 27 * C, 2 * Z), F32)],
            compiler_params=pltpu.CompilerParams(vmem_limit_bytes=32 << 20),
            cost_estimate=pl.CostEstimate(flops=4000000000, bytes_accessed=6000000, transcendentals=0),
        )(own, band1, band2, bias1, bias2)
        parts = pl.pallas_call(
            outer_kernel,
            out_shape=jax.ShapeDtypeStruct((S * S * ROWS, Z), BF),
            in_specs=[SMEM] + [VMEM] * 11,
            out_specs=VMEM,
            scratch_shapes=[
                pltpu.VMEM((6, XQ, C, Z), BF),
                pltpu.VMEM((6, XQ * C, Z), BF),
                pltpu.VMEM((XQ + 2, YQ + 2, C, Z), BF),
                pltpu.VMEM((2, 27 * C, 2 * Z), F32),
            ],
            compiler_params=pltpu.CompilerParams(vmem_limit_bytes=32 << 20),
            cost_estimate=pl.CostEstimate(flops=5000000000, bytes_accessed=7000000, transcendentals=0),
        )(place, own, low, high, far, one, two, band1, band2, bias1, bias2, head)

        back = swap(parts.reshape(S * S, ROWS, Z)).reshape(S * S * ROWS, Z)
        return pl.pallas_call(
            finish_kernel,
            out_shape=jax.ShapeDtypeStruct((S, 2 * S, Z), F32),
            in_specs=[VMEM, VMEM, SMEM],
            out_specs=VMEM,
            compiler_params=pltpu.CompilerParams(vmem_limit_bytes=16 << 20),
        )(back, jnp.asarray(pick_matrix()), b_last)

    return body


def solution(mesh):
    rows, steps = mesh.shape["inline"], mesh.shape["crosslin"]
    groups = [
        [i * steps + x * LINE + l for l in range(LINE) for i in range(rows)] for x in range(steps // LINE)
    ]
    far_pairs = []
    for i in range(rows):
        for at in range(steps - LINE):
            below, above = i * steps + at, i * steps + at + LINE
            if i % S == 0:
                far_pairs.append((above, below))
            if i % S == S - 1:
                far_pairs.append((below, above))
    return jax.shard_map(
        make_body(groups, far_pairs, steps),
        mesh=mesh,
        in_specs=(P(None, "inline", "crosslin", None), P(), P(), P(), P(), P(), P()),
        out_specs=P("inline", "crosslin", None),
        check_vma=False,
    )
```

```python
import jax
import jax.numpy as jnp
import numpy as np
from jax import lax
from jax.experimental import pallas as pl
from jax.experimental.pallas import tpu as pltpu
from jax.sharding import PartitionSpec as P

S = 8
C = 32
XQ = 16
YQ = 8
Z = 128
LINE = 4
HALF = 8 * C
ROWS = 24
BF = jnp.bfloat16
F32 = jnp.float32


def split_kernel(in_ref, out_ref, arrived, rows, sorted_, sems, out_sems):
    copies = [pltpu.make_async_copy(in_ref.at[:, x], arrived.at[x], sems.at[x]) for x in range(S)]
    for copy in copies:
        copy.start()
    leaving = []
    for x in range(S):
        copies[x].wait()
        rows[x % 2] = arrived[x].reshape(2 * S * C, Z).astype(F32)
        for phase in range(S):
            for step in range(2):
                value = rows[x % 2, pl.ds(step * S + phase, C, stride=2 * S), :]
                sorted_[x, phase, step * C : (step + 1) * C, :] = value.astype(BF)
        leave = pltpu.make_async_copy(sorted_.at[x], out_ref.at[x * S : (x + 1) * S], out_sems.at[x])
        leave.start()
        leaving.append(leave)
    for leave in leaving:
        leave.wait()


def band_kernel(w1_ref, w2_ref, o1_ref, o2_ref):
    row = lax.broadcasted_iota(jnp.int32, (C, HALF), 0)
    lane = lax.broadcasted_iota(jnp.int32, (C, HALF), 1)
    repeat = jnp.where(lax.rem(lane, C) == row, 1.0, 0.0).astype(BF)
    block = lane // C
    for w_ref, o_ref in ((w1_ref, o1_ref), (w2_ref, o2_ref)):
        for dy in range(3):
            for dz in range(3):
                taps = [
                    jnp.dot(
                        w_ref[((a * 3 + dy) * 3 + dz) * C : ((a * 3 + dy) * 3 + dz + 1) * C, :],
                        repeat,
                        preferred_element_type=F32,
                    )
                    for a in range(3)
                ]
                for p in range(10):
                    value = jnp.zeros((C, HALF), F32)
                    for a in range(3):
                        if 0 <= p + a - 2 < 8:
                            value = jnp.where(block == p + a - 2, taps[a], value)
                    at = (dz * 10 + p) * C
                    o_ref[at : at + C, dy * HALF : (dy + 1) * HALF] = value.astype(BF)


def finish_layer(part, steps, bias, keep):
    lane = lax.broadcasted_iota(jnp.int32, (C, Z), 1)
    for x in range(XQ):
        for step in range(steps):
            taps = []
            for dz in range(3):
                found = [part(h, dz, x - 7 * h, step) for h in range(2) if 0 <= x - 7 * h <= 8]
                taps.append(found[0] if len(found) == 1 else found[0] + found[1])
            total = taps[1] + jnp.where(lane < S, 0.0, pltpu.roll(taps[0], S, 1))
            total = total + jnp.where(lane >= Z - S, 0.0, pltpu.roll(taps[2], Z - S, 1))
            keep(x, step, jnp.maximum(total + bias, 0.0))


def layer_pair(fetch, first, second, w_ref, b_ref, sums, keep):
    for h in range(2):
        taps = jnp.concatenate(
            [w_ref[(dz * 10 + 1 - h) * C : (dz * 10 + 10 - h) * C, :] for dz in range(3)], axis=0
        )
        window = jnp.concatenate(
            [
                jnp.concatenate([fetch(first + dy, h), fetch(second + dy, h)], axis=1)
                for dy in (-1, 0, 1)
            ],
            axis=0,
        )
        sums[h] = jnp.dot(taps, window, preferred_element_type=F32)

    def part(h, dz, x, step):
        at = (dz * 9 + x) * C
        return sums[h, at : at + C, step * Z : (step + 1) * Z]

    finish_layer(part, 2, b_ref[...], lambda x, step, value: keep(x, (first, second)[step], value))


def layer_one(fetch, w_ref, b_ref, sums, keep):
    window = jnp.concatenate(
        [jnp.concatenate([fetch(dy, 0), fetch(dy, 1)], axis=1) for dy in (-1, 0, 1)], axis=0
    )
    sums[...] = jnp.dot(w_ref[...], window, preferred_element_type=F32)

    def part(h, dz, x, step):
        at = (dz * 10 + x + 1 - h) * C
        return sums[at : at + C, h * Z : (h + 1) * Z]

    finish_layer(part, 1, b_ref[...], lambda x, step, value: keep(x, value))


def inner_kernel(own_ref, w1_ref, w2_ref, b1_ref, b2_ref, one_ref, two_ref, sums):
    def features(y, h):
        return own_ref[y // 2, h * 8 : h * 8 + 8, y % 2].reshape(HALF, Z)

    def hidden(y, h):
        return one_ref[y - 1, h * HALF : (h + 1) * HALF, :]

    def keep_one(x, y, value):
        one_ref[y - 1, x * C : (x + 1) * C, :] = value.astype(BF)

    def keep_two(x, y, value):
        two_ref[x, y - 2] = value.astype(BF)

    for y in range(1, 4):
        layer_pair(features, y, y + 3, w1_ref, b1_ref, sums, keep_one)
    for y in range(2, 4):
        layer_pair(hidden, y, y + 2, w2_ref, b2_ref, sums, keep_two)


def outer_kernel(
    place_ref, own_ref, low_ref, high_ref, far_ref, one_ref, two_ref, w1_ref, w2_ref, b1_ref, b2_ref, head_ref,
    out_ref, ends, edge, h2s, planes, sums, single,
):
    block, dx, ext, start = place_ref[0], place_ref[1], place_ref[2], place_ref[3]
    not_first = jnp.where(block > 0, 1.0, 0.0)
    not_last = jnp.where(block < 3, 1.0, 0.0)
    ninth = jnp.where(start == 0, not_first, not_last)

    def inside(y, value):
        return value * not_first if y < 0 else value * not_last if y >= YQ else value

    def slot(y):
        return y + 3 if y < 0 else y - 5

    for x in range(XQ):
        ends[0, x] = far_ref[x]
        ends[5, x] = far_ref[x]
        for y in range(2):
            ends[1 + y, x] = low_ref[x, y]
            ends[3 + y, x] = high_ref[x, y]

    def features(y, h):
        part = slice(h * 8, h * 8 + 8)
        value = own_ref[y // 2, part, y % 2] if 0 <= y < YQ else ends[slot(y), part]
        return value.reshape(HALF, Z)

    def hidden(y, h):
        part = slice(h * HALF, (h + 1) * HALF)
        if 1 <= y <= 6:
            return one_ref[y - 1, part, :]
        return edge[y + 2 if y < 1 else y - 4, part, :]

    def keep_one(x, y, value):
        edge[y + 2 if y < 1 else y - 4, x * C : (x + 1) * C, :] = inside(y, value).astype(BF)

    def keep_two(x, y, value):
        h2s[x + 1, y + 1] = value.astype(BF)

    def keep_one_ninth(x, value):
        edge[jnp.where(start == 0, 0, 5), x * C : (x + 1) * C, :] = (value * ninth).astype(BF)

    def keep_two_ninth(x, value):
        h2s[x + 1, jnp.where(start == 0, 0, 9)] = (value * ninth).astype(BF)

    for y in (-1, 0):
        layer_pair(features, y, y + 8, w1_ref, b1_ref, sums, keep_one)
    layer_one(
        lambda dy, h: ends[start + 1 + dy, h * 8 : h * 8 + 8].reshape(HALF, Z), w1_ref, b1_ref, single, keep_one_ninth
    )
    h2s[0] = jnp.zeros((YQ + 2, C, Z), BF)
    h2s[XQ + 1] = jnp.zeros((YQ + 2, C, Z), BF)
    for x in range(XQ):
        h2s[x + 1, 3:7] = two_ref[x]
    for y in (0, 1):
        layer_pair(hidden, y, y + 6, w2_ref, b2_ref, sums, keep_two)
    layer_one(
        lambda dy, h: edge[start + 1 + dy, h * HALF : (h + 1) * HALF, :], w2_ref, b2_ref, single, keep_two_ninth
    )

    lane = lax.broadcasted_iota(jnp.int32, (2 * ROWS, Z), 1)
    planes[0] = jnp.zeros((LINE, ROWS, Z), F32)
    planes[XQ + 1] = jnp.zeros((LINE, ROWS, Z), F32)
    for x in range(1, XQ + 1, 2):
        for l in range(0, LINE, 2):
            columns = []
            for k in (l, l + 1):
                y = 2 * k + 1
                columns.append(
                    jnp.concatenate([h2s[at, step] for at in (x, x + 1) for step in (y, y + 1, y + ext)], axis=0)
                )
            both = jnp.dot(head_ref[...], jnp.concatenate(columns, axis=1), preferred_element_type=F32)
            for k in range(2):
                part = both[:, k * Z : (k + 1) * Z]
                before = jnp.where(lane < 1, 0.0, pltpu.roll(part[: 2 * ROWS], 1, 1))
                after = jnp.where(lane >= Z - 1, 0.0, pltpu.roll(part[4 * ROWS :], Z - 1, 1))
                total = part[2 * ROWS : 4 * ROWS] + before + after
                planes[x, l + k] = total[:ROWS]
                planes[x + 1, l + k] = total[ROWS:]
    moved = lax.rem(lax.broadcasted_iota(jnp.int32, (ROWS, Z), 0), 9) // 3 == dx + 1
    for l in range(LINE):
        for x in range(1, XQ + 1, 2):
            rows = [jnp.where(moved, planes[at + dx, l], planes[at, l]) for at in (x, x + 1)]
            at = (l * XQ + x - 1) * ROWS
            out_ref[at : at + 2 * ROWS, :] = jnp.concatenate(rows, axis=0).astype(BF)


def finish_kernel(back_ref, pick_ref, b_ref, out_ref):
    totals = [None] * S
    for r in range(S):
        sums = jnp.dot(
            pick_ref[...], back_ref[r * S * ROWS : (r + 1) * S * ROWS, :], preferred_element_type=F32
        )
        for a in range(3):
            to = (r - (a - 1)) % S
            part = sums[a * 16 : (a + 1) * 16]
            totals[to] = part if totals[to] is None else totals[to] + part
    for x in range(S):
        out_ref[x] = 1.0 / (1.0 + jnp.exp(-(totals[x] + b_ref[0])))


def pick_matrix():
    pick = np.zeros((3, 2, S, S, ROWS), np.float32)
    for a in range(3):
        for e in range(2):
            for y in range(S):
                for b in range(3):
                    pick[a, e, y, (y + b - 1) % S, e * 9 + a * 3 + b] = 1.0
    return pick.reshape(3 * 2 * S, S * ROWS).astype(jnp.bfloat16)


def head_matrix(w_last, s):
    b = jnp.arange(3)[None, :]
    e = jnp.arange(2)[:, None]
    up = (b == 2) & (s == 0)
    down = (b == 0) & (s == S - 1)
    source = jnp.where(up, e + 1, jnp.where(down, jnp.where(e == 0, 2, 0), e))
    mask = (source[..., None] == jnp.arange(3)).astype(BF)
    weight = jnp.transpose(w_last, (2, 0, 1, 3))
    full = mask[None, :, None, :, :, None] * weight[:, None, :, :, None, :]
    full = jnp.pad(full.reshape(3, 18, 3 * C), ((0, 0), (0, ROWS - 18), (0, 0)))
    zero = jnp.zeros_like(full)
    pair = jnp.stack([jnp.concatenate([full, zero], axis=2), jnp.concatenate([zero, full], axis=2)], axis=1)
    return pair.reshape(6 * ROWS, 6 * C)


VMEM = pl.BlockSpec(memory_space=pltpu.VMEM)
SMEM = pl.BlockSpec(memory_space=pltpu.SMEM)


def make_body(groups, far_pairs, steps):
    axes = ("inline", "crosslin")

    def swap(value):
        return lax.all_to_all(value, axes, 0, 0, tiled=True, axis_index_groups=groups)

    def body(features, w1, b1, w2, b2, w_last, b_last):
        j = lax.axis_index("crosslin")
        block = j // LINE
        k = lax.rem(j, LINE) * XQ + lax.axis_index("inline")
        r, s = k // S, lax.rem(k, S)

        send = pl.pallas_call(
            split_kernel,
            out_shape=jax.ShapeDtypeStruct((S * S, 2 * C, Z), BF),
            in_specs=[pl.BlockSpec(memory_space=pltpu.HBM)],
            out_specs=pl.BlockSpec(memory_space=pltpu.HBM),
            scratch_shapes=[
                pltpu.VMEM((S, C, 2 * S, Z), BF),
                pltpu.VMEM((2, 2 * S * C, Z), F32),
                pltpu.VMEM((S, S, 2 * C, Z), BF),
                pltpu.SemaphoreType.DMA((S,)),
                pltpu.SemaphoreType.DMA((S,)),
            ],
            compiler_params=pltpu.CompilerParams(vmem_limit_bytes=60 << 20),
        )(features)
        own = swap(send)
        band1, band2 = pl.pallas_call(
            band_kernel,
            out_shape=[jax.ShapeDtypeStruct((30 * C, 3 * HALF), BF)] * 2,
            in_specs=[VMEM] * 2,
            out_specs=[VMEM] * 2,
            compiler_params=pltpu.CompilerParams(vmem_limit_bytes=16 << 20),
            cost_estimate=pl.CostEstimate(flops=60000000, bytes_accessed=3200000, transcendentals=0),
        )(w1.reshape(27 * C, C), w2.reshape(27 * C, C))
        dx = jnp.where(r == 0, 1, jnp.where(r == S - 1, -1, 0))
        ext = jnp.where(s == S - 1, -1, 2)
        place = jnp.stack([block, dx, ext, jnp.where(s == S - 1, 0, 3)]).astype(jnp.int32)
        head = head_matrix(w_last, s)
        bias1, bias2 = (jnp.broadcast_to(b[:, None], (C, Z)) for b in (b1, b2))
        own, band1, band2, place, head, bias1, bias2 = lax.optimization_barrier(
            (own, band1, band2, place, head, bias1, bias2)
        )

        own = own.reshape(LINE, XQ, 2, C, Z)
        far = jnp.where(s == S - 1, own[2, :, 1], own[1, :, 0])
        high = lax.ppermute(own[0], "crosslin", [(i + LINE, i) for i in range(steps - LINE)])
        low = lax.ppermute(own[3], "crosslin", [(i, i + LINE) for i in range(steps - LINE)])
        far = lax.ppermute(far, axes, far_pairs)

        one, two = pl.pallas_call(
            inner_kernel,
            out_shape=[jax.ShapeDtypeStruct((6, XQ * C, Z), BF), jax.ShapeDtypeStruct((XQ, 4, C, Z), BF)],
            in_specs=[VMEM] * 5,
            out_specs=[VMEM] * 2,
            scratch_shapes=[pltpu.VMEM((2, 27 * C, 2 * Z), F32)],
            compiler_params=pltpu.CompilerParams(vmem_limit_bytes=32 << 20),
            cost_estimate=pl.CostEstimate(flops=4000000000, bytes_accessed=6000000, transcendentals=0),
        )(own, band1, band2, bias1, bias2)
        parts = pl.pallas_call(
            outer_kernel,
            out_shape=jax.ShapeDtypeStruct((S * S * ROWS, Z), BF),
            in_specs=[SMEM] + [VMEM] * 11,
            out_specs=VMEM,
            scratch_shapes=[
                pltpu.VMEM((6, XQ, C, Z), BF),
                pltpu.VMEM((6, XQ * C, Z), BF),
                pltpu.VMEM((XQ + 2, YQ + 2, C, Z), BF),
                pltpu.VMEM((XQ + 2, LINE, ROWS, Z), F32),
                pltpu.VMEM((2, 27 * C, 2 * Z), F32),
                pltpu.VMEM((30 * C, 2 * Z), F32),
            ],
            compiler_params=pltpu.CompilerParams(vmem_limit_bytes=32 << 20),
            cost_estimate=pl.CostEstimate(flops=5000000000, bytes_accessed=7000000, transcendentals=0),
        )(place, own, low, high, far, one, two, band1, band2, bias1, bias2, head)

        back = swap(parts.reshape(S * S, ROWS, Z)).reshape(S * S * ROWS, Z)
        return pl.pallas_call(
            finish_kernel,
            out_shape=jax.ShapeDtypeStruct((S, 2 * S, Z), F32),
            in_specs=[VMEM, VMEM, SMEM],
            out_specs=VMEM,
            compiler_params=pltpu.CompilerParams(vmem_limit_bytes=16 << 20),
        )(back, jnp.asarray(pick_matrix()), b_last)

    return body


def solution(mesh):
    rows, steps = mesh.shape["inline"], mesh.shape["crosslin"]
    groups = [
        [i * steps + x * LINE + l for l in range(LINE) for i in range(rows)] for x in range(steps // LINE)
    ]
    far_pairs = []
    for i in range(rows):
        for at in range(steps - LINE):
            below, above = i * steps + at, i * steps + at + LINE
            if i % S == 0:
                far_pairs.append((above, below))
            if i % S == S - 1:
                far_pairs.append((below, above))
    return jax.shard_map(
        make_body(groups, far_pairs, steps),
        mesh=mesh,
        in_specs=(P(None, "inline", "crosslin", None), P(), P(), P(), P(), P(), P()),
        out_specs=P("inline", "crosslin", None),
        check_vma=False,
    )
```

```python
import jax
import jax.numpy as jnp
import numpy as np
from jax import lax
from jax.experimental import pallas as pl
from jax.experimental.pallas import tpu as pltpu
from jax.sharding import PartitionSpec as P

S = 8
C = 32
XQ = 16
YQ = 8
Z = 128
LINE = 4
HALF = 8 * C
ROWS = 24
BF = jnp.bfloat16
F32 = jnp.float32


def split_kernel(in_ref, out_ref, arrived, rows, sorted_, sems, out_sems):
    copies = [pltpu.make_async_copy(in_ref.at[:, x], arrived.at[x], sems.at[x]) for x in range(S)]
    for copy in copies:
        copy.start()
    leaving = []
    for x in range(S):
        copies[x].wait()
        rows[x % 2] = arrived[x].reshape(2 * S * C, Z).astype(F32)
        for phase in range(S):
            for step in range(2):
                value = rows[x % 2, pl.ds(step * S + phase, C, stride=2 * S), :]
                sorted_[x, phase, step * C : (step + 1) * C, :] = value.astype(BF)
        leave = pltpu.make_async_copy(sorted_.at[x], out_ref.at[x * S : (x + 1) * S], out_sems.at[x])
        leave.start()
        leaving.append(leave)
    for leave in leaving:
        leave.wait()


def band_kernel(w1_ref, w2_ref, o1_ref, o2_ref):
    row = lax.broadcasted_iota(jnp.int32, (C, HALF), 0)
    lane = lax.broadcasted_iota(jnp.int32, (C, HALF), 1)
    repeat = jnp.where(lax.rem(lane, C) == row, 1.0, 0.0).astype(BF)
    block = lane // C
    for w_ref, o_ref in ((w1_ref, o1_ref), (w2_ref, o2_ref)):
        for dy in range(3):
            for dz in range(3):
                taps = [
                    jnp.dot(
                        w_ref[((a * 3 + dy) * 3 + dz) * C : ((a * 3 + dy) * 3 + dz + 1) * C, :],
                        repeat,
                        preferred_element_type=F32,
                    )
                    for a in range(3)
                ]
                for p in range(10):
                    value = jnp.zeros((C, HALF), F32)
                    for a in range(3):
                        if 0 <= p + a - 2 < 8:
                            value = jnp.where(block == p + a - 2, taps[a], value)
                    at = (dz * 10 + p) * C
                    o_ref[at : at + C, dy * HALF : (dy + 1) * HALF] = value.astype(BF)


def finish_layer(part, steps, bias, keep):
    lane = lax.broadcasted_iota(jnp.int32, (C, Z), 1)
    for x in range(XQ):
        for step in range(steps):
            taps = []
            for dz in range(3):
                found = [part(h, dz, x - 7 * h, step) for h in range(2) if 0 <= x - 7 * h <= 8]
                taps.append(found[0] if len(found) == 1 else found[0] + found[1])
            total = taps[1] + jnp.where(lane < S, 0.0, pltpu.roll(taps[0], S, 1))
            total = total + jnp.where(lane >= Z - S, 0.0, pltpu.roll(taps[2], Z - S, 1))
            keep(x, step, jnp.maximum(total + bias, 0.0))


def layer_pair(fetch, first, second, w_ref, b_ref, sums, keep):
    for h in range(2):
        taps = jnp.concatenate(
            [w_ref[(dz * 10 + 1 - h) * C : (dz * 10 + 10 - h) * C, :] for dz in range(3)], axis=0
        )
        window = jnp.concatenate(
            [
                jnp.concatenate([fetch(first + dy, h), fetch(second + dy, h)], axis=1)
                for dy in (-1, 0, 1)
            ],
            axis=0,
        )
        sums[h] = jnp.dot(taps, window, preferred_element_type=F32)

    def part(h, dz, x, step):
        at = (dz * 9 + x) * C
        return sums[h, at : at + C, step * Z : (step + 1) * Z]

    finish_layer(part, 2, b_ref[...], lambda x, step, value: keep(x, (first, second)[step], value))


def layer_one(fetch, w_ref, b_ref, sums, keep):
    window = jnp.concatenate(
        [jnp.concatenate([fetch(dy, 0), fetch(dy, 1)], axis=1) for dy in (-1, 0, 1)], axis=0
    )
    sums[...] = jnp.dot(w_ref[...], window, preferred_element_type=F32)

    def part(h, dz, x, step):
        at = (dz * 10 + x + 1 - h) * C
        return sums[at : at + C, h * Z : (h + 1) * Z]

    finish_layer(part, 1, b_ref[...], lambda x, step, value: keep(x, value))


def inner_kernel(own_ref, w1_ref, w2_ref, b1_ref, b2_ref, one_ref, two_ref, sums):
    def features(y, h):
        return own_ref[y // 2, h * 8 : h * 8 + 8, y % 2].reshape(HALF, Z)

    def hidden(y, h):
        return one_ref[y - 1, h * HALF : (h + 1) * HALF, :]

    def keep_one(x, y, value):
        one_ref[y - 1, x * C : (x + 1) * C, :] = value.astype(BF)

    def keep_two(x, y, value):
        two_ref[x, y - 2] = value.astype(BF)

    for y in range(1, 4):
        layer_pair(features, y, y + 3, w1_ref, b1_ref, sums, keep_one)
    for y in range(2, 4):
        layer_pair(hidden, y, y + 2, w2_ref, b2_ref, sums, keep_two)


def outer_kernel(
    place_ref, own_ref, low_ref, high_ref, far_ref, one_ref, two_ref, w1_ref, w2_ref, b1_ref, b2_ref, head_ref,
    out_ref, ends, edge, h2s, planes, sums, single, message, sems,
):
    block, dx, ext, start = place_ref[0], place_ref[1], place_ref[2], place_ref[3]
    not_first = jnp.where(block > 0, 1.0, 0.0)
    not_last = jnp.where(block < 3, 1.0, 0.0)
    ninth = jnp.where(start == 0, not_first, not_last)

    def inside(y, value):
        return value * not_first if y < 0 else value * not_last if y >= YQ else value

    def slot(y):
        return y + 3 if y < 0 else y - 5

    for x in range(XQ):
        ends[0, x] = far_ref[x]
        ends[5, x] = far_ref[x]
        for y in range(2):
            ends[1 + y, x] = low_ref[x, y]
            ends[3 + y, x] = high_ref[x, y]

    def features(y, h):
        part = slice(h * 8, h * 8 + 8)
        value = own_ref[y // 2, part, y % 2] if 0 <= y < YQ else ends[slot(y), part]
        return value.reshape(HALF, Z)

    def hidden(y, h):
        part = slice(h * HALF, (h + 1) * HALF)
        if 1 <= y <= 6:
            return one_ref[y - 1, part, :]
        return edge[y + 2 if y < 1 else y - 4, part, :]

    def keep_one(x, y, value):
        edge[y + 2 if y < 1 else y - 4, x * C : (x + 1) * C, :] = inside(y, value).astype(BF)

    def keep_two(x, y, value):
        h2s[x + 1, y + 1] = value.astype(BF)

    def keep_one_ninth(x, value):
        edge[jnp.where(start == 0, 0, 5), x * C : (x + 1) * C, :] = (value * ninth).astype(BF)

    def keep_two_ninth(x, value):
        h2s[x + 1, jnp.where(start == 0, 0, 9)] = (value * ninth).astype(BF)

    for y in (-1, 0):
        layer_pair(features, y, y + 8, w1_ref, b1_ref, sums, keep_one)
    layer_one(
        lambda dy, h: ends[start + 1 + dy, h * 8 : h * 8 + 8].reshape(HALF, Z), w1_ref, b1_ref, single, keep_one_ninth
    )
    h2s[0] = jnp.zeros((YQ + 2, C, Z), BF)
    h2s[XQ + 1] = jnp.zeros((YQ + 2, C, Z), BF)
    for x in range(XQ):
        h2s[x + 1, 3:7] = two_ref[x]
    for y in (0, 1):
        layer_pair(hidden, y, y + 6, w2_ref, b2_ref, sums, keep_two)
    layer_one(
        lambda dy, h: edge[start + 1 + dy, h * HALF : (h + 1) * HALF, :], w2_ref, b2_ref, single, keep_two_ninth
    )

    lane = lax.broadcasted_iota(jnp.int32, (2 * ROWS, Z), 1)
    planes[0] = jnp.zeros((LINE, ROWS, Z), F32)
    planes[XQ + 1] = jnp.zeros((LINE, ROWS, Z), F32)
    moved = lax.rem(lax.broadcasted_iota(jnp.int32, (ROWS, Z), 0), 9) // 3 == dx + 1
    leaving = []
    for l in range(0, LINE, 2):
        for x in range(1, XQ + 1, 2):
            columns = []
            for k in (l, l + 1):
                y = 2 * k + 1
                columns.append(
                    jnp.concatenate([h2s[at, step] for at in (x, x + 1) for step in (y, y + 1, y + ext)], axis=0)
                )
            both = jnp.dot(head_ref[...], jnp.concatenate(columns, axis=1), preferred_element_type=F32)
            for k in range(2):
                part = both[:, k * Z : (k + 1) * Z]
                before = jnp.where(lane < 1, 0.0, pltpu.roll(part[: 2 * ROWS], 1, 1))
                after = jnp.where(lane >= Z - 1, 0.0, pltpu.roll(part[4 * ROWS :], Z - 1, 1))
                total = part[2 * ROWS : 4 * ROWS] + before + after
                planes[x, l + k] = total[:ROWS]
                planes[x + 1, l + k] = total[ROWS:]
        for k in (l, l + 1):
            for x in range(1, XQ + 1, 2):
                rows = [jnp.where(moved, planes[at + dx, k], planes[at, k]) for at in (x, x + 1)]
                at = (k * XQ + x - 1) * ROWS
                message[at : at + 2 * ROWS, :] = jnp.concatenate(rows, axis=0).astype(BF)
        part = pl.ds(l * XQ * ROWS, 2 * XQ * ROWS)
        leave = pltpu.make_async_copy(message.at[part], out_ref.at[part], sems.at[l // 2])
        leave.start()
        leaving.append(leave)
    for leave in leaving:
        leave.wait()


def finish_kernel(back_ref, pick_ref, b_ref, out_ref):
    totals = [None] * S
    for r in range(S):
        sums = jnp.dot(
            pick_ref[...], back_ref[r * S * ROWS : (r + 1) * S * ROWS, :], preferred_element_type=F32
        )
        for a in range(3):
            to = (r - (a - 1)) % S
            part = sums[a * 16 : (a + 1) * 16]
            totals[to] = part if totals[to] is None else totals[to] + part
    for x in range(S):
        out_ref[x] = 1.0 / (1.0 + jnp.exp(-(totals[x] + b_ref[0])))


def pick_matrix():
    pick = np.zeros((3, 2, S, S, ROWS), np.float32)
    for a in range(3):
        for e in range(2):
            for y in range(S):
                for b in range(3):
                    pick[a, e, y, (y + b - 1) % S, e * 9 + a * 3 + b] = 1.0
    return pick.reshape(3 * 2 * S, S * ROWS).astype(jnp.bfloat16)


def head_matrix(w_last, s):
    b = jnp.arange(3)[None, :]
    e = jnp.arange(2)[:, None]
    up = (b == 2) & (s == 0)
    down = (b == 0) & (s == S - 1)
    source = jnp.where(up, e + 1, jnp.where(down, jnp.where(e == 0, 2, 0), e))
    mask = (source[..., None] == jnp.arange(3)).astype(BF)
    weight = jnp.transpose(w_last, (2, 0, 1, 3))
    full = mask[None, :, None, :, :, None] * weight[:, None, :, :, None, :]
    full = jnp.pad(full.reshape(3, 18, 3 * C), ((0, 0), (0, ROWS - 18), (0, 0)))
    zero = jnp.zeros_like(full)
    pair = jnp.stack([jnp.concatenate([full, zero], axis=2), jnp.concatenate([zero, full], axis=2)], axis=1)
    return pair.reshape(6 * ROWS, 6 * C)


VMEM = pl.BlockSpec(memory_space=pltpu.VMEM)
SMEM = pl.BlockSpec(memory_space=pltpu.SMEM)


def make_body(groups, far_pairs, steps):
    axes = ("inline", "crosslin")

    def swap(value):
        return lax.all_to_all(value, axes, 0, 0, tiled=True, axis_index_groups=groups)

    def body(features, w1, b1, w2, b2, w_last, b_last):
        j = lax.axis_index("crosslin")
        block = j // LINE
        k = lax.rem(j, LINE) * XQ + lax.axis_index("inline")
        r, s = k // S, lax.rem(k, S)

        send = pl.pallas_call(
            split_kernel,
            out_shape=jax.ShapeDtypeStruct((S * S, 2 * C, Z), BF),
            in_specs=[pl.BlockSpec(memory_space=pltpu.HBM)],
            out_specs=pl.BlockSpec(memory_space=pltpu.HBM),
            scratch_shapes=[
                pltpu.VMEM((S, C, 2 * S, Z), BF),
                pltpu.VMEM((2, 2 * S * C, Z), F32),
                pltpu.VMEM((S, S, 2 * C, Z), BF),
                pltpu.SemaphoreType.DMA((S,)),
                pltpu.SemaphoreType.DMA((S,)),
            ],
            compiler_params=pltpu.CompilerParams(vmem_limit_bytes=60 << 20),
        )(features)
        own = swap(send)
        band1, band2 = pl.pallas_call(
            band_kernel,
            out_shape=[jax.ShapeDtypeStruct((30 * C, 3 * HALF), BF)] * 2,
            in_specs=[VMEM] * 2,
            out_specs=[VMEM] * 2,
            compiler_params=pltpu.CompilerParams(vmem_limit_bytes=16 << 20),
            cost_estimate=pl.CostEstimate(flops=60000000, bytes_accessed=3200000, transcendentals=0),
        )(w1.reshape(27 * C, C), w2.reshape(27 * C, C))
        dx = jnp.where(r == 0, 1, jnp.where(r == S - 1, -1, 0))
        ext = jnp.where(s == S - 1, -1, 2)
        place = jnp.stack([block, dx, ext, jnp.where(s == S - 1, 0, 3)]).astype(jnp.int32)
        head = head_matrix(w_last, s)
        bias1, bias2 = (jnp.broadcast_to(b[:, None], (C, Z)) for b in (b1, b2))
        own, band1, band2, place, head, bias1, bias2 = lax.optimization_barrier(
            (own, band1, band2, place, head, bias1, bias2)
        )

        own = own.reshape(LINE, XQ, 2, C, Z)
        far = jnp.where(s == S - 1, own[2, :, 1], own[1, :, 0])
        high = lax.ppermute(own[0], "crosslin", [(i + LINE, i) for i in range(steps - LINE)])
        low = lax.ppermute(own[3], "crosslin", [(i, i + LINE) for i in range(steps - LINE)])
        far = lax.ppermute(far, axes, far_pairs)

        one, two = pl.pallas_call(
            inner_kernel,
            out_shape=[jax.ShapeDtypeStruct((6, XQ * C, Z), BF), jax.ShapeDtypeStruct((XQ, 4, C, Z), BF)],
            in_specs=[VMEM] * 5,
            out_specs=[VMEM] * 2,
            scratch_shapes=[pltpu.VMEM((2, 27 * C, 2 * Z), F32)],
            compiler_params=pltpu.CompilerParams(vmem_limit_bytes=32 << 20),
            cost_estimate=pl.CostEstimate(flops=4000000000, bytes_accessed=6000000, transcendentals=0),
        )(own, band1, band2, bias1, bias2)
        parts = pl.pallas_call(
            outer_kernel,
            out_shape=jax.ShapeDtypeStruct((S * S * ROWS, Z), BF),
            in_specs=[SMEM] + [VMEM] * 11,
            out_specs=pl.BlockSpec(memory_space=pltpu.HBM),
            scratch_shapes=[
                pltpu.VMEM((6, XQ, C, Z), BF),
                pltpu.VMEM((6, XQ * C, Z), BF),
                pltpu.VMEM((XQ + 2, YQ + 2, C, Z), BF),
                pltpu.VMEM((XQ + 2, LINE, ROWS, Z), F32),
                pltpu.VMEM((2, 27 * C, 2 * Z), F32),
                pltpu.VMEM((30 * C, 2 * Z), F32),
                pltpu.VMEM((S * S * ROWS, Z), BF),
                pltpu.SemaphoreType.DMA((2,)),
            ],
            compiler_params=pltpu.CompilerParams(vmem_limit_bytes=32 << 20),
            cost_estimate=pl.CostEstimate(flops=5000000000, bytes_accessed=7000000, transcendentals=0),
        )(place, own, low, high, far, one, two, band1, band2, bias1, bias2, head)

        back = swap(parts.reshape(S * S, ROWS, Z)).reshape(S * S * ROWS, Z)
        return pl.pallas_call(
            finish_kernel,
            out_shape=jax.ShapeDtypeStruct((S, 2 * S, Z), F32),
            in_specs=[VMEM, VMEM, SMEM],
            out_specs=VMEM,
            compiler_params=pltpu.CompilerParams(vmem_limit_bytes=16 << 20),
        )(back, jnp.asarray(pick_matrix()), b_last)

    return body


def solution(mesh):
    rows, steps = mesh.shape["inline"], mesh.shape["crosslin"]
    groups = [
        [i * steps + x * LINE + l for l in range(LINE) for i in range(rows)] for x in range(steps // LINE)
    ]
    far_pairs = []
    for i in range(rows):
        for at in range(steps - LINE):
            below, above = i * steps + at, i * steps + at + LINE
            if i % S == 0:
                far_pairs.append((above, below))
            if i % S == S - 1:
                far_pairs.append((below, above))
    return jax.shard_map(
        make_body(groups, far_pairs, steps),
        mesh=mesh,
        in_specs=(P(None, "inline", "crosslin", None), P(), P(), P(), P(), P(), P()),
        out_specs=P("inline", "crosslin", None),
        check_vma=False,
    )
```
